32 devices in a mesh: cube: 2 (over core), row: 4 (over y, x), col: 4 (over z).
Axes of the slice: x: 2, y: 2, z: 4, core: 2. Of those that a mesh axis runs over, the one named last changes fastest.
Arguments:
- child_update: float32 [2, 8192, 8192], P('cube', 'row', 'col'), may hold values from -8 to 80, as said below
- child_panel: bfloat16 [2, 8192, 2048], P('cube', 'row'), may hold values from -8 to 8
- parent_front: bfloat16 [16384, 16384], P('row', ('cube', 'col')), may hold values from -8 to 520, as said below
- block_map: int32 [2, 64], replicated, may hold values from 0 to 127, as said below
Outputs:
- schur: float32 [16384, 16384], P('row', ('cube', 'col'))
- panel: float32 [16384, 512], P('row')
The draws below stay inside these ranges and needn't reach their ends.
Inputs may be any that keep to these rules, and one draw needn't show every extreme that they name: child_update[k] is symmetric for every child. parent_front is symmetric, and the leading 512 x 512 block of front is positive definite. `block_map`: for each child the 64 entries are distinct. Split a child's entries into aligned groups of 16 entries. In every group, for each r from 0 to 3, exactly 4 entries e have e // 32 equal to r. In every group, at most 2 entries share one value of e // 16, and every group has a value shared by 2 entries.
All inputs are finite; a program needn't handle non-finite values.
Results may differ from the reference program's by a relative error of at most 0.00044.
Values may be sent and summed in bfloat16 or wider, within the bound.
A program may use at most 320 MiB of HBM per device.

```python
import math
import jax
import jax.numpy as jnp

CONTRIB = 8192
PARENT = 16384
BLK = 128
PANEL = 512
KW = 2048
CHILDREN = 2
CHILD_BLOCKS = 64
PARENT_BLOCKS = 128


fine_rows = 8


fine_cols = 16


def panel_fan():
    return max(1, KW // 64)


def draw_child_panel(key, part):
    shape_all = (CHILDREN, CONTRIB, KW)
    spread = 1.0 / math.sqrt(panel_fan())
    raw_draw = jnp.clip(jax.random.normal(key, shape_all, jnp.float32), -6.0, 6.0)
    return (raw_draw * spread).astype(jnp.bfloat16)


def draw_child_update(key, part):
    shape_all = (CHILDREN, CONTRIB, CONTRIB)
    raw_draw = jnp.clip(jax.random.normal(key, shape_all, jnp.float32), -5.6, 5.6)
    symmetric = (raw_draw + jnp.swapaxes(raw_draw, 1, 2)) * 0.7071
    base_shift = float(KW // panel_fan())
    shifts = jax.random.uniform(jax.random.fold_in(key, 11), (CHILDREN, CONTRIB), jnp.float32, base_shift + 2.0, base_shift + 8.0)
    indices = jnp.arange(CONTRIB)
    symmetric = symmetric.at[:, indices, indices].add(shifts)
    return symmetric.astype(jnp.float32)


def draw_parent_front(key, part):
    shape_pair = (PARENT, PARENT)
    raw_draw = jnp.clip(jax.random.normal(key, shape_pair, jnp.float32), -5.6, 5.6)
    symmetric = (raw_draw + raw_draw.T) * 0.7071
    pivot_low = 2 * (KW + 2 * PANEL) // panel_fan() + PANEL // 4 + 16
    pivot_high = pivot_low + pivot_low // 2
    pivot_part = jax.random.uniform(jax.random.fold_in(key, 7), (PARENT,), jnp.float32, float(pivot_low), float(pivot_high))
    other_part = jax.random.uniform(jax.random.fold_in(key, 9), (PARENT,), jnp.float32, 4.0, 12.0)
    indices = jnp.arange(PARENT)
    diagonal = jnp.where(indices < PANEL, pivot_part, other_part)
    symmetric = symmetric.at[indices, indices].add(diagonal)
    return symmetric.astype(jnp.bfloat16)


def child_map(key):
    total_blocks = CONTRIB // BLK
    parent_blocks = PARENT // BLK
    group_size = total_blocks // fine_rows
    group_count = total_blocks // group_size
    span_cols = parent_blocks // fine_cols
    split_keys = jax.random.split(key, 3)
    group_ids = jnp.arange(group_count, dtype=jnp.int32)[:, None]
    member_ids = jnp.arange(group_size, dtype=jnp.int32)[None, :]
    row_range = jnp.broadcast_to(member_ids % fine_rows, (group_count, group_size))
    flip_bits = jax.random.randint(split_keys[0], (group_count, group_size), 0, 2, dtype=jnp.int32)
    column_range = 2 * row_range + flip_bits
    offset_rank = jnp.broadcast_to(group_ids, (group_count, group_size))
    orders = jax.vmap(lambda sub_key: jax.random.permutation(sub_key, span_cols))(jax.random.split(split_keys[1], fine_cols))
    position = orders[column_range, offset_rank]
    target = span_cols * column_range + position
    shuffles = jax.vmap(lambda sub_key: jax.random.permutation(sub_key, group_size))(jax.random.split(split_keys[2], group_count))
    mapped = jnp.take_along_axis(target, shuffles, axis=1)
    return mapped.reshape(total_blocks).astype(jnp.int32)


def draw_block_map(key, part):
    return jax.vmap(child_map)(jax.random.split(key, CHILDREN)).astype(jnp.int32)


def setup_inputs(seed: int = 0) -> dict:
    streams_of = jax.random.split(jax.random.key(seed), 5)
    return {
        "child_update": draw_child_update(jax.random.fold_in(streams_of[4], 71), 0),
        "child_panel": draw_child_panel(jax.random.fold_in(streams_of[4], 71), 0),
        "parent_front": draw_parent_front(jax.random.fold_in(streams_of[4], 71), 0),
        "block_map": draw_block_map(jax.random.fold_in(streams_of[4], 71), 0),
    }


def reference(child_update, child_panel, parent_front, block_map):
    front_full = parent_front.astype(jnp.float32)
    block_tiles = front_full.reshape(PARENT_BLOCKS, BLK, PARENT_BLOCKS, BLK).transpose(0, 2, 1, 3)
    for member in range(CHILDREN):
        factor_rows = child_panel[member]
        contrib = child_update[member] - jnp.dot(factor_rows.astype(jnp.float32), factor_rows.T.astype(jnp.float32), preferred_element_type=jnp.float32)
        pieces = contrib.reshape(CHILD_BLOCKS, BLK, CHILD_BLOCKS, BLK).transpose(0, 2, 1, 3)
        where_to = block_map[member].astype(jnp.int32)
        block_tiles = block_tiles.at[where_to[:, None], where_to[None, :]].add(pieces)
    front_full = block_tiles.transpose(0, 2, 1, 3).reshape(PARENT, PARENT)
    pivot_factor = jnp.linalg.cholesky(front_full[:PANEL, :PANEL])
    solved = jax.scipy.linalg.solve_triangular(pivot_factor, front_full[PANEL:, :PANEL].T, lower=True).T
    panel_full = jnp.concatenate([pivot_factor, solved], axis=0)
    panel_low = panel_full.astype(jnp.bfloat16)
    update_full = front_full - jnp.dot(panel_low.astype(jnp.float32), panel_low.T.astype(jnp.float32), preferred_element_type=jnp.float32)
    indices = jnp.arange(PARENT)
    keep_mask = (indices[:, None] >= PANEL) & (indices[None, :] >= PANEL)
    schur_full = jnp.where(keep_mask, update_full, jnp.zeros_like(update_full))
    return (schur_full, panel_full)
```

```python
import functools

import jax
import jax.numpy as jnp
from jax import lax
from jax.experimental import pallas as pl
from jax.experimental.pallas import tpu as pltpu
from jax.sharding import PartitionSpec as P

BLK = 128
PANEL = 512
WIRE = jnp.float16
SHRINK = 1.0 / 4.0
FRONT_SHRINK = 1.0 / 8.0
HIGHEST = lax.Precision.HIGHEST


def group_ranks(labels):
    position = jnp.arange(labels.shape[-1])
    before = position[:, None] > position[None, :]
    same_label = labels[..., :, None] == labels[..., None, :]
    return jnp.sum(jnp.logical_and(same_label, before), axis=-1)


def member_of_slot(slot, slots, count):
    hits = (slot[:, None] == jnp.arange(slots)).astype(jnp.int32)
    return jnp.sum(hits * jnp.arange(count, dtype=jnp.int32)[:, None], axis=0)


def slot_of_block(grouped, slot_in_group, cap, first, count):
    groups = grouped.shape[1]
    wanted = first + jnp.arange(count, dtype=jnp.int32)
    hits = grouped[..., None] == wanted
    value = jnp.arange(groups, dtype=jnp.int32)[None, :, None] * cap + slot_in_group
    total = jnp.sum(jnp.where(hits, value[..., None] + 1, 0), axis=(1, 2))
    return total.astype(jnp.int32) - 1


def pack_kernel(slots, tables, rows_ref, panel_ref, update_ref, out_ref, held):
    cubes, cols, cap = slots
    product = lax.dot_general(
        rows_ref[...], panel_ref[...], (((1,), (1,)), ((), ())), preferred_element_type=jnp.float32
    )
    held[...] = (update_ref[...] - product) * SHRINK
    count = pl.num_programs(0)
    for cube in range(cubes):
        for col in range(cols):
            for rank in range(cap):
                slot = (cube * cols + col) * cap + rank
                start = pl.multiple_of(tables[count + slot] * BLK, BLK)
                out_ref[cube, 0, col, :, rank * BLK : (rank + 1) * BLK] = held[
                    :, pl.ds(start, BLK)
                ]


def pack(own_panel, column_panel, update, my_rows, my_cols, sizes):
    cubes, rows, cols, row_cap, col_cap = sizes
    group_blocks = update.shape[0] // BLK
    width = update.shape[1]
    depth = own_panel.shape[1]
    tables = jnp.concatenate([my_rows, my_cols]).astype(jnp.int32)
    return pl.pallas_call(
        functools.partial(pack_kernel, (cubes, cols, col_cap)),
        out_shape=jax.ShapeDtypeStruct(
            (cubes, rows, cols, row_cap * BLK, col_cap * BLK), jnp.float32
        ),
        grid_spec=pltpu.PrefetchScalarGridSpec(
            num_scalar_prefetch=1,
            grid=(group_blocks,),
            in_specs=[
                pl.BlockSpec((BLK, depth), lambda s, t: (t[s], 0)),
                pl.BlockSpec((width, depth), lambda s, t: (0, 0)),
                pl.BlockSpec((BLK, width), lambda s, t: (t[s], 0)),
            ],
            out_specs=pl.BlockSpec(
                (cubes, 1, cols, BLK, col_cap * BLK),
                lambda s, t: (0, s // row_cap, 0, s % row_cap, 0),
            ),
            scratch_shapes=[pltpu.VMEM((BLK, width), jnp.float32)],
        ),
        compiler_params=pltpu.CompilerParams(vmem_limit_bytes=50 * 2**20),
        name="pack",
    )(tables, own_panel, column_panel, update)


def front_block(tables, layout, parent_ref, arrived, block):
    range_rows, range_cols, col_cap = layout
    children = len(arrived)
    step = pl.program_id(0)
    total = parent_ref[:, block * BLK : (block + 1) * BLK].astype(jnp.float32)
    for child, ref in enumerate(arrived):
        row_slot = tables[child * range_rows + step]
        col_slot = tables[children * range_rows + child * range_cols + block]
        slot = jnp.maximum(col_slot, 0)
        start = pl.multiple_of((slot % col_cap) * BLK, BLK)
        piece = ref[0, 0, slot // col_cap, :, pl.ds(start, BLK)]
        factor = jnp.where((row_slot >= 0) & (col_slot >= 0), 1.0 / SHRINK, 0.0)
        total = total + piece * factor
    return total


def strip_kernel(layout, blocks, tables, parent_ref, *refs):
    arrived, out_ref = refs[:-1], refs[-1]
    for block in range(blocks):
        out_ref[:, block * BLK : (block + 1) * BLK] = front_block(
            tables, layout, parent_ref, arrived, block
        )


def final_kernel(layout, blocks, tables, parent_ref, rows_ref, cols_ref, *refs):
    arrived, out_ref = refs[:-1], refs[-1]
    range_rows, range_cols, col_cap = layout
    children = len(arrived)
    base = children * (range_rows + range_cols)
    first_row, first_col = tables[base], tables[base + 1]
    row_ok = first_row + pl.program_id(0) >= PANEL // BLK
    product = jnp.dot(rows_ref[...], cols_ref[...], preferred_element_type=jnp.float32)
    for block in range(blocks):
        total = front_block(tables, layout, parent_ref, arrived, block)
        keep = row_ok & (first_col + block >= PANEL // BLK)
        left = total - product[:, block * BLK : (block + 1) * BLK]
        out_ref[:, block * BLK : (block + 1) * BLK] = jnp.where(keep, left, 0.0)


def over_front(kernel, name, tables, parent, arrived, extras, extra_specs, row_blocks, col_blocks):
    children, rows, cols, high, wide = arrived.shape
    row_cap, col_cap = high // BLK, wide // BLK
    range_rows, range_cols = parent.shape[0] // BLK, parent.shape[1] // BLK
    width = col_blocks * BLK

    def source(child):
        def index(step, t):
            slot = jnp.maximum(t[child * range_rows + step], 0)
            return (child, slot // row_cap, 0, slot % row_cap, 0)

        return pl.BlockSpec((1, 1, cols, BLK, wide), index)

    return pl.pallas_call(
        functools.partial(kernel, (range_rows, range_cols, col_cap), col_blocks),
        out_shape=jax.ShapeDtypeStruct((row_blocks * BLK, width), jnp.float32),
        grid_spec=pltpu.PrefetchScalarGridSpec(
            num_scalar_prefetch=1,
            grid=(row_blocks,),
            in_specs=[pl.BlockSpec((BLK, width), lambda s, t: (s, 0))]
            + extra_specs
            + [source(child) for child in range(children)],
            out_specs=pl.BlockSpec((BLK, width), lambda s, t: (s, 0)),
        ),
        compiler_params=pltpu.CompilerParams(vmem_limit_bytes=50 * 2**20),
        name=name,
    )(tables, parent, *extras, *([arrived] * children))


def factor_pivot(pivot):
    steps = PANEL // BLK
    left = [
        [pivot[i * BLK : (i + 1) * BLK, j * BLK : (j + 1) * BLK] for j in range(i + 1)]
        for i in range(steps)
    ]
    factor = [[None] * steps for _ in range(steps)]
    inverses = []
    unit = jnp.eye(BLK, dtype=jnp.float32)
    for j in range(steps):
        factor[j][j] = jnp.linalg.cholesky(left[j][j], symmetrize_input=False)
        inverse = jax.scipy.linalg.solve_triangular(factor[j][j], unit, lower=True)
        inverses.append(inverse)
        for i in range(j + 1, steps):
            factor[i][j] = jnp.dot(left[i][j], inverse.T, precision=HIGHEST)
        for i in range(j + 1, steps):
            for m in range(j + 1, i + 1):
                left[i][m] = left[i][m] - jnp.dot(factor[i][j], factor[m][j].T, precision=HIGHEST)
    return factor, inverses


def solve_cols(factor, inverses, top):
    done = []
    for j in range(PANEL // BLK):
        right = top[j * BLK : (j + 1) * BLK]
        if j:
            known = jnp.concatenate(factor[j][:j], axis=1)
            right = right - jnp.dot(known, jnp.concatenate(done, axis=0), precision=HIGHEST)
        done.append(jnp.dot(inverses[j], right, precision=HIGHEST))
    return jnp.concatenate(done, axis=0)


def solve_rows(factor, inverses, strip):
    done = []
    for j in range(PANEL // BLK):
        right = strip[:, j * BLK : (j + 1) * BLK]
        if j:
            known = jnp.concatenate(factor[j][:j], axis=1)
            right = right - jnp.dot(jnp.concatenate(done, axis=1), known.T, precision=HIGHEST)
        done.append(jnp.dot(right, inverses[j].T, precision=HIGHEST))
    return jnp.concatenate(done, axis=1)


def body(child_update, child_panel, parent_front, block_map):
    grid_rows = lax.axis_size("row")
    cube_count = lax.axis_size("cube")
    col_count = lax.axis_size("col")
    grid_cols = cube_count * col_count
    child_index = lax.axis_index("cube")
    row_index = lax.axis_index("row")
    col_index = lax.axis_index("col")
    range_index = lax.axis_index(("cube", "col"))
    group_blocks = child_update.shape[1] // BLK
    row_cap = group_blocks // grid_rows
    col_cap = max(1, group_blocks // grid_cols)
    front_rows, front_cols = parent_front.shape
    range_rows = front_rows // BLK
    range_cols = front_cols // BLK

    own_panel = child_panel[0]
    share = own_panel.shape[0] // col_count
    piece = lax.dynamic_slice_in_dim(own_panel, col_index * share, share, 0)
    swap = [
        (r * col_count + c, c * col_count + r) for r in range(grid_rows) for c in range(col_count)
    ]
    piece = lax.ppermute(piece, ("row", "col"), swap)
    column_panel = lax.all_gather(piece, "row", axis=0, tiled=True)

    children = block_map.shape[0]
    grouped = block_map.reshape(children, grid_rows, group_blocks)
    row_dest = grouped // range_rows
    col_dest = grouped // range_cols
    row_slot = row_dest * row_cap + group_ranks(row_dest)
    col_rank = group_ranks(col_dest)
    row_rank = row_slot - row_dest * row_cap
    col_slot = col_dest * col_cap + col_rank
    my_rows = member_of_slot(row_slot[child_index, row_index], group_blocks, group_blocks)
    my_cols = member_of_slot(col_slot[child_index, col_index], grid_cols * col_cap, group_blocks)
    from_rows = slot_of_block(grouped, row_rank, row_cap, row_index * range_rows, range_rows)
    from_cols = slot_of_block(grouped, col_rank, col_cap, range_index * range_cols, range_cols)
    tables = jnp.concatenate(
        [
            from_rows.reshape(-1),
            from_cols.reshape(-1),
            jnp.stack([row_index * range_rows, range_index * range_cols]),
        ]
    ).astype(jnp.int32)

    packed = pack(
        own_panel,
        column_panel,
        child_update[0],
        my_rows,
        my_cols,
        (cube_count, grid_rows, col_count, row_cap, col_cap),
    )
    shape = packed.shape
    packed = packed.astype(WIRE)
    arrived = lax.all_to_all(
        packed.reshape((-1,) + shape[3:]),
        ("cube", "row", "col"),
        split_axis=0,
        concat_axis=0,
        tiled=True,
    )
    arrived = arrived.astype(jnp.float32).reshape(shape)

    panel_blocks = PANEL // BLK
    strip = over_front(
        strip_kernel, "strip", tables, parent_front, arrived, [], [], range_rows, panel_blocks
    )
    top = over_front(
        strip_kernel, "top", tables, parent_front, arrived, [], [], panel_blocks, range_cols
    )
    corner = (row_index == 0) & (range_index == 0)
    pivot = lax.psum(jnp.where(corner, strip[:PANEL], 0.0), ("cube", "row", "col"))
    top_low = jnp.where(row_index == 0, top * FRONT_SHRINK, 0.0).astype(WIRE)
    strip_low = jnp.where(range_index == 0, strip * FRONT_SHRINK, 0.0).astype(WIRE)
    top_all = lax.psum(top_low, "row").astype(jnp.float32) * (1.0 / FRONT_SHRINK)
    strip_all = lax.psum(strip_low, ("cube", "col")).astype(jnp.float32) * (1.0 / FRONT_SHRINK)

    factor, inverses = factor_pivot(pivot)
    cols_low = solve_cols(factor, inverses, top_all).astype(jnp.bfloat16)
    solved = solve_rows(factor, inverses, strip_all)
    zero = jnp.zeros((BLK, BLK), jnp.float32)
    lower = jnp.concatenate(
        [
            jnp.concatenate(
                [factor[i][j] if j <= i else zero for j in range(panel_blocks)], axis=1
            )
            for i in range(panel_blocks)
        ],
        axis=0,
    )
    head = jnp.where(row_index == 0, lower, solved[:PANEL])
    panel_rows = lax.dynamic_update_slice(solved, head, (0, 0))
    rows_low = panel_rows.astype(jnp.bfloat16)
    schur = over_front(
        final_kernel,
        "final",
        tables,
        parent_front,
        arrived,
        [rows_low, cols_low],
        [
            pl.BlockSpec((BLK, PANEL), lambda s, t: (s, 0)),
            pl.BlockSpec((PANEL, front_cols), lambda s, t: (0, 0)),
        ],
        range_rows,
        range_cols,
    )
    return (schur, panel_rows)


def solution(mesh):
    placed = (P("cube", "row", "col"), P("cube", "row", None), P("row", ("cube", "col")), P())
    return jax.shard_map(
        body,
        mesh=mesh,
        in_specs=placed,
        out_specs=(P("row", ("cube", "col")), P("row", None)),
        check_vma=False,
    )
```

```python
import functools

import jax
import jax.numpy as jnp
from jax import lax
from jax.experimental import pallas as pl
from jax.experimental.pallas import tpu as pltpu
from jax.sharding import PartitionSpec as P

BLK = 128
PANEL = 512
WIRE = jnp.float16
SHRINK = 1.0 / 4.0
FRONT_SHRINK = 1.0 / 8.0
HIGHEST = lax.Precision.HIGHEST


def group_ranks(labels):
    position = jnp.arange(labels.shape[-1])
    before = position[:, None] > position[None, :]
    same_label = labels[..., :, None] == labels[..., None, :]
    return jnp.sum(jnp.logical_and(same_label, before), axis=-1)


def member_of_slot(slot, slots, count):
    hits = (slot[:, None] == jnp.arange(slots)).astype(jnp.int32)
    return jnp.sum(hits * jnp.arange(count, dtype=jnp.int32)[:, None], axis=0)


def slot_of_block(grouped, slot_in_group, cap, first, count):
    groups = grouped.shape[1]
    wanted = first + jnp.arange(count, dtype=jnp.int32)
    hits = grouped[..., None] == wanted
    value = jnp.arange(groups, dtype=jnp.int32)[None, :, None] * cap + slot_in_group
    total = jnp.sum(jnp.where(hits, value[..., None] + 1, 0), axis=(1, 2))
    return total.astype(jnp.int32) - 1


def spread(block, axes):
    count = lax.axis_size(axes)
    copies = jnp.broadcast_to(block[None], (count,) + block.shape)
    joined = lax.all_to_all(copies, axes, split_axis=0, concat_axis=0, tiled=True)
    return joined.reshape((-1,) + block.shape[1:])


def broadcast(block, axes):
    count = lax.axis_size(axes)
    shares = block.reshape((count, -1) + block.shape[1:])
    return spread(lax.all_to_all(shares, axes, split_axis=0, concat_axis=0, tiled=True)[0], axes)


def pack_kernel(slots, tables, rows_ref, panel_ref, update_ref, out_ref, held):
    cubes, cols, cap = slots
    product = lax.dot_general(
        rows_ref[...], panel_ref[...], (((1,), (1,)), ((), ())), preferred_element_type=jnp.float32
    )
    held[...] = (update_ref[...] - product) * SHRINK
    count = pl.num_programs(0)
    for cube in range(cubes):
        for col in range(cols):
            for rank in range(cap):
                slot = (cube * cols + col) * cap + rank
                start = pl.multiple_of(tables[count + slot] * BLK, BLK)
                out_ref[cube, 0, col, :, rank * BLK : (rank + 1) * BLK] = held[
                    :, pl.ds(start, BLK)
                ]


def pack(own_panel, column_panel, update, my_rows, my_cols, sizes):
    cubes, rows, cols, row_cap, col_cap = sizes
    group_blocks = update.shape[0] // BLK
    width = update.shape[1]
    depth = own_panel.shape[1]
    tables = jnp.concatenate([my_rows, my_cols]).astype(jnp.int32)
    return pl.pallas_call(
        functools.partial(pack_kernel, (cubes, cols, col_cap)),
        out_shape=jax.ShapeDtypeStruct(
            (cubes, rows, cols, row_cap * BLK, col_cap * BLK), jnp.float32
        ),
        grid_spec=pltpu.PrefetchScalarGridSpec(
            num_scalar_prefetch=1,
            grid=(group_blocks,),
            in_specs=[
                pl.BlockSpec((BLK, depth), lambda s, t: (t[s], 0)),
                pl.BlockSpec((width, depth), lambda s, t: (0, 0)),
                pl.BlockSpec((BLK, width), lambda s, t: (t[s], 0)),
            ],
            out_specs=pl.BlockSpec(
                (cubes, 1, cols, BLK, col_cap * BLK),
                lambda s, t: (0, s // row_cap, 0, s % row_cap, 0),
            ),
            scratch_shapes=[pltpu.VMEM((BLK, width), jnp.float32)],
        ),
        compiler_params=pltpu.CompilerParams(vmem_limit_bytes=50 * 2**20),
        name="pack",
    )(tables, own_panel, column_panel, update)


def front_block(tables, layout, parent_ref, arrived, block):
    range_rows, range_cols, col_cap = layout
    children = len(arrived)
    step = pl.program_id(0)
    total = parent_ref[:, block * BLK : (block + 1) * BLK].astype(jnp.float32)
    for child, ref in enumerate(arrived):
        row_slot = tables[child * range_rows + step]
        col_slot = tables[children * range_rows + child * range_cols + block]
        slot = jnp.maximum(col_slot, 0)
        start = pl.multiple_of((slot % col_cap) * BLK, BLK)
        piece = ref[0, 0, slot // col_cap, :, pl.ds(start, BLK)]
        factor = jnp.where((row_slot >= 0) & (col_slot >= 0), 1.0 / SHRINK, 0.0)
        total = total + piece * factor
    return total


def strip_kernel(layout, blocks, tables, parent_ref, *refs):
    arrived, out_ref = refs[:-1], refs[-1]
    for block in range(blocks):
        out_ref[:, block * BLK : (block + 1) * BLK] = front_block(
            tables, layout, parent_ref, arrived, block
        )


def final_kernel(layout, blocks, tables, parent_ref, rows_ref, cols_ref, *refs):
    arrived, out_ref = refs[:-1], refs[-1]
    range_rows, range_cols, col_cap = layout
    children = len(arrived)
    base = children * (range_rows + range_cols)
    first_row, first_col = tables[base], tables[base + 1]
    row_ok = first_row + pl.program_id(0) >= PANEL // BLK
    product = jnp.dot(rows_ref[...], cols_ref[...], preferred_element_type=jnp.float32)
    for block in range(blocks):
        total = front_block(tables, layout, parent_ref, arrived, block)
        keep = row_ok & (first_col + block >= PANEL // BLK)
        left = total - product[:, block * BLK : (block + 1) * BLK]
        out_ref[:, block * BLK : (block + 1) * BLK] = jnp.where(keep, left, 0.0)


def over_front(kernel, name, tables, parent, arrived, extras, extra_specs, row_blocks, col_blocks):
    children, rows, cols, high, wide = arrived.shape
    row_cap, col_cap = high // BLK, wide // BLK
    range_rows, range_cols = parent.shape[0] // BLK, parent.shape[1] // BLK
    width = col_blocks * BLK

    def source(child):
        def index(step, t):
            slot = jnp.maximum(t[child * range_rows + step], 0)
            return (child, slot // row_cap, 0, slot % row_cap, 0)

        return pl.BlockSpec((1, 1, cols, BLK, wide), index)

    return pl.pallas_call(
        functools.partial(kernel, (range_rows, range_cols, col_cap), col_blocks),
        out_shape=jax.ShapeDtypeStruct((row_blocks * BLK, width), jnp.float32),
        grid_spec=pltpu.PrefetchScalarGridSpec(
            num_scalar_prefetch=1,
            grid=(row_blocks,),
            in_specs=[pl.BlockSpec((BLK, width), lambda s, t: (s, 0))]
            + extra_specs
            + [source(child) for child in range(children)],
            out_specs=pl.BlockSpec((BLK, width), lambda s, t: (s, 0)),
        ),
        compiler_params=pltpu.CompilerParams(vmem_limit_bytes=50 * 2**20),
        name=name,
    )(tables, parent, *extras, *([arrived] * children))


def factor_pivot(pivot):
    steps = PANEL // BLK
    left = [
        [pivot[i * BLK : (i + 1) * BLK, j * BLK : (j + 1) * BLK] for j in range(i + 1)]
        for i in range(steps)
    ]
    factor = [[None] * steps for _ in range(steps)]
    inverses = []
    unit = jnp.eye(BLK, dtype=jnp.float32)
    for j in range(steps):
        factor[j][j] = jnp.linalg.cholesky(left[j][j], symmetrize_input=False)
        inverse = jax.scipy.linalg.solve_triangular(factor[j][j], unit, lower=True)
        inverses.append(inverse)
        for i in range(j + 1, steps):
            factor[i][j] = jnp.dot(left[i][j], inverse.T, precision=HIGHEST)
        for i in range(j + 1, steps):
            for m in range(j + 1, i + 1):
                left[i][m] = left[i][m] - jnp.dot(factor[i][j], factor[m][j].T, precision=HIGHEST)
    return factor, inverses


def solve_cols(factor, inverses, top):
    done = []
    for j in range(PANEL // BLK):
        right = top[j * BLK : (j + 1) * BLK]
        if j:
            known = jnp.concatenate(factor[j][:j], axis=1)
            right = right - jnp.dot(known, jnp.concatenate(done, axis=0), precision=HIGHEST)
        done.append(jnp.dot(inverses[j], right, precision=HIGHEST))
    return jnp.concatenate(done, axis=0)


def solve_rows(factor, inverses, strip):
    done = []
    for j in range(PANEL // BLK):
        right = strip[:, j * BLK : (j + 1) * BLK]
        if j:
            known = jnp.concatenate(factor[j][:j], axis=1)
            right = right - jnp.dot(jnp.concatenate(done, axis=1), known.T, precision=HIGHEST)
        done.append(jnp.dot(right, inverses[j].T, precision=HIGHEST))
    return jnp.concatenate(done, axis=1)


def body(child_update, child_panel, parent_front, block_map):
    grid_rows = lax.axis_size("row")
    cube_count = lax.axis_size("cube")
    col_count = lax.axis_size("col")
    grid_cols = cube_count * col_count
    child_index = lax.axis_index("cube")
    row_index = lax.axis_index("row")
    col_index = lax.axis_index("col")
    range_index = lax.axis_index(("cube", "col"))
    group_blocks = child_update.shape[1] // BLK
    row_cap = group_blocks // grid_rows
    col_cap = max(1, group_blocks // grid_cols)
    front_rows, front_cols = parent_front.shape
    range_rows = front_rows // BLK
    range_cols = front_cols // BLK

    own_panel = child_panel[0]
    share = own_panel.shape[0] // col_count
    piece = lax.dynamic_slice_in_dim(own_panel, col_index * share, share, 0)
    swap = [
        (r * col_count + c, c * col_count + r) for r in range(grid_rows) for c in range(col_count)
    ]
    piece = lax.ppermute(piece, ("row", "col"), swap)
    column_panel = spread(piece, "row")

    children = block_map.shape[0]
    grouped = block_map.reshape(children, grid_rows, group_blocks)
    row_dest = grouped // range_rows
    col_dest = grouped // range_cols
    row_slot = row_dest * row_cap + group_ranks(row_dest)
    col_rank = group_ranks(col_dest)
    row_rank = row_slot - row_dest * row_cap
    col_slot = col_dest * col_cap + col_rank
    my_rows = member_of_slot(row_slot[child_index, row_index], group_blocks, group_blocks)
    my_cols = member_of_slot(col_slot[child_index, col_index], grid_cols * col_cap, group_blocks)
    from_rows = slot_of_block(grouped, row_rank, row_cap, row_index * range_rows, range_rows)
    from_cols = slot_of_block(grouped, col_rank, col_cap, range_index * range_cols, range_cols)
    tables = jnp.concatenate(
        [
            from_rows.reshape(-1),
            from_cols.reshape(-1),
            jnp.stack([row_index * range_rows, range_index * range_cols]),
        ]
    ).astype(jnp.int32)

    packed = pack(
        own_panel,
        column_panel,
        child_update[0],
        my_rows,
        my_cols,
        (cube_count, grid_rows, col_count, row_cap, col_cap),
    )
    shape = packed.shape
    packed = packed.astype(WIRE)
    arrived = lax.all_to_all(
        packed.reshape((-1,) + shape[3:]),
        ("cube", "row", "col"),
        split_axis=0,
        concat_axis=0,
        tiled=True,
    )
    arrived = arrived.astype(jnp.float32).reshape(shape)

    panel_blocks = PANEL // BLK
    strip = over_front(
        strip_kernel, "strip", tables, parent_front, arrived, [], [], range_rows, panel_blocks
    )
    top = over_front(
        strip_kernel, "top", tables, parent_front, arrived, [], [], panel_blocks, range_cols
    )
    pivot = broadcast(strip[:PANEL], ("cube", "row", "col"))
    top_low, strip_low, pivot = lax.optimization_barrier(
        ((top * FRONT_SHRINK).astype(WIRE), (strip * FRONT_SHRINK).astype(WIRE), pivot)
    )
    top_all = broadcast(top_low, "row").astype(jnp.float32) * (1.0 / FRONT_SHRINK)
    strip_all = broadcast(strip_low, ("cube", "col")).astype(jnp.float32) * (1.0 / FRONT_SHRINK)

    factor, inverses = factor_pivot(pivot)
    cols_low = solve_cols(factor, inverses, top_all).astype(jnp.bfloat16)
    solved = solve_rows(factor, inverses, strip_all)
    zero = jnp.zeros((BLK, BLK), jnp.float32)
    lower = jnp.concatenate(
        [
            jnp.concatenate(
                [factor[i][j] if j <= i else zero for j in range(panel_blocks)], axis=1
            )
            for i in range(panel_blocks)
        ],
        axis=0,
    )
    head = jnp.where(row_index == 0, lower, solved[:PANEL])
    panel_rows = lax.dynamic_update_slice(solved, head, (0, 0))
    rows_low = panel_rows.astype(jnp.bfloat16)
    schur = over_front(
        final_kernel,
        "final",
        tables,
        parent_front,
        arrived,
        [rows_low, cols_low],
        [
            pl.BlockSpec((BLK, PANEL), lambda s, t: (s, 0)),
            pl.BlockSpec((PANEL, front_cols), lambda s, t: (0, 0)),
        ],
        range_rows,
        range_cols,
    )
    return (schur, panel_rows)


def solution(mesh):
    placed = (P("cube", "row", "col"), P("cube", "row", None), P("row", ("cube", "col")), P())
    return jax.shard_map(
        body,
        mesh=mesh,
        in_specs=placed,
        out_specs=(P("row", ("cube", "col")), P("row", None)),
        check_vma=False,
    )
```
